32 devices in a mesh: lsec: 8 (over z, x), rsec: 4 (over y, core).
Axes of the slice: x: 2, y: 2, z: 4, core: 2. Of those that a mesh axis runs over, the one named last changes fastest.
Arguments:
- states: float32 [2, 5120, 2560], P(None, 'lsec', 'rsec'), may hold values from -6 to 6
- left_env: float32 [8, 640, 640], P('lsec', 'rsec'), may hold values from -0.25 to 0.25
- right_env: float32 [4, 640, 640], P('rsec', 'lsec'), may hold values from -0.25 to 0.25
- left_op: float32 [8, 640, 640], P('lsec', 'rsec'), may hold values from -0.25 to 0.25
- right_op: float32 [4, 640, 640], P('rsec', 'lsec'), may hold values from -0.25 to 0.25
- sizes_left: int32 [8], P('lsec'), may hold values from 320 to 640
- sizes_right: int32 [4], P('rsec'), may hold values from 320 to 640
Outputs:
- applied: float32 [2, 5120, 2560], P(None, 'lsec', 'rsec')
The draws below stay inside these ranges and needn't reach their ends.
All inputs are finite; a program needn't handle non-finite values.
Results may differ from the reference program's by a relative error of at most 0.000059.
Values sent between devices are 32-bit elements; how exact they have to be, the bound alone decides.
No kernel may reach another device: no remote copies, remote signals or barrier semaphores. Data moves between devices by JAX's collectives and lax.ppermute only.
A program may use at most 128 MiB of HBM per device.

```python
import jax
import jax.numpy as jnp
from jax import lax

CAP = 640
ROOTS = 2
SEC_L = 8
SEC_R = 4


def touch_ends(array, rng, smallest, largest):
    place = [jax.random.randint(jax.random.fold_in(rng, axis), (), 0, length) for axis, length in enumerate(array.shape)]
    main_axis = array.shape.index(max(array.shape))
    beside = place[:main_axis] + [(place[main_axis] + 1) % array.shape[main_axis]] + place[main_axis + 1:]
    return array.at[tuple(place)].set(smallest).at[tuple(beside)].set(largest)


def block_scale(stream_key, extent, pieces, least, high):
    gain = 1.0
    for position, parts in pieces:
        draws = jax.random.uniform(jax.random.fold_in(jax.random.fold_in(stream_key, 6), position), (parts,), jnp.float32, least / len(pieces), high / len(pieces))
        gain = gain * jnp.repeat(jnp.exp(draws), extent[position] // parts).reshape((-1,) + (1,) * (len(extent) - 1 - position))
    return gain


def noise(own_key, dims, spread, limit, shards=(), kind=jnp.bfloat16):
    drawn = jax.random.normal(own_key, dims, jnp.float32) * spread
    if len(shards) > 0:
        drawn = block_scale(own_key, dims, shards, -0.22, 0.18) * drawn
    return jnp.clip(drawn, min=-limit, max=limit).astype(kind)


def setup_inputs(seed: int = 0) -> dict:
    key_of = jax.random.split(jax.random.key(seed), 8)
    states = noise(key_of[0], (ROOTS, SEC_L * CAP, SEC_R * CAP), 1.0, 6.0, ((1, 8), (2, 4)), jnp.float32)
    left_env = noise(key_of[1], (SEC_L, CAP, CAP), CAP ** -0.5, 0.25, ((0, 8), (1, 4)), jnp.float32)
    right_env = noise(key_of[2], (SEC_R, CAP, CAP), CAP ** -0.5, 0.25, ((0, 4), (1, 8)), jnp.float32)
    left_op = noise(key_of[3], (SEC_L, CAP, CAP), CAP ** -0.5, 0.25, ((0, 8), (1, 4)), jnp.float32)
    right_op = noise(key_of[4], (SEC_R, CAP, CAP), CAP ** -0.5, 0.25, ((0, 4), (1, 8)), jnp.float32)
    sizes_left = touch_ends(jax.random.randint(key_of[5], (SEC_L,), CAP // 2, CAP + 1), jax.random.fold_in(key_of[5], 1), CAP // 2, CAP).astype(jnp.int32)
    sizes_right = touch_ends(jax.random.randint(key_of[6], (SEC_R,), CAP // 2, CAP + 1), jax.random.fold_in(key_of[6], 1), CAP // 2, CAP).astype(jnp.int32)
    return dict(states=states, left_env=left_env, right_env=right_env, left_op=left_op, right_op=right_op, sizes_left=sizes_left, sizes_right=sizes_right)


HI = lax.Precision.HIGHEST


def reference(states, left_env, right_env, left_op, right_op, sizes_left, sizes_right):
    rows = jnp.arange(CAP, dtype=jnp.int32)
    mask_l = (rows[None, :] < sizes_left[:, None]).astype(jnp.float32)
    mask_r = (rows[None, :] < sizes_right[:, None]).astype(jnp.float32)
    mask = mask_l[:, :, None, None] * mask_r[None, None, :, :]
    blocks = states.reshape(ROOTS, SEC_L, CAP, SEC_R, CAP) * mask[None]
    local = jnp.einsum('iab,ribjc->riajc', left_env, blocks, precision=HI)
    local = local + jnp.einsum('ribjc,jdc->ribjd', blocks, right_env, precision=HI)
    moved = jnp.pad(blocks[:, :-1, :, 1:, :], ((0, 0), (1, 0), (0, 0), (0, 1), (0, 0)))
    inner = jnp.einsum('ribjc,jdc->ribjd', moved, right_op, precision=HI)
    hop = jnp.einsum('iab,ribjd->riajd', left_op, inner, precision=HI)
    right_part = jnp.einsum('ribjc,jcd->ribjd', blocks, right_op, precision=HI)
    source = jnp.einsum('iba,ribjd->riajd', left_op, right_part, precision=HI)
    back = jnp.pad(source[:, 1:, :, :-1, :], ((0, 0), (0, 1), (0, 0), (1, 0), (0, 0)))
    applied = (local + hop + back) * mask[None]
    return applied.reshape(ROOTS, SEC_L * CAP, SEC_R * CAP)
```

```python
import functools

import jax
import jax.numpy as jnp
from jax import lax
from jax.experimental import pallas as pl
from jax.experimental.pallas import tpu as pltpu
from jax.sharding import PartitionSpec as P

AXES = ("lsec", "rsec")
CHUNKS = 4
F32, BF16 = jnp.float32, jnp.bfloat16
VMEM_LIMIT = 48 * 1024 * 1024


def split(x):
    hi = x.astype(BF16)
    return hi, (x - hi.astype(F32)).astype(BF16)


def dot_nn(a, b):
    left = jnp.concatenate([a[0], a[0], a[1]], axis=1)
    right = jnp.concatenate([b[0], b[1], b[0]], axis=0)
    return lax.dot_general(left, right, (((1,), (0,)), ((), ())), preferred_element_type=F32)


def dot_nt(a, b):
    left = jnp.concatenate([a[0], a[0], a[1]], axis=1)
    right = jnp.concatenate([b[0], b[1], b[0]], axis=1)
    return lax.dot_general(left, right, (((1,), (1,)), ((), ())), preferred_element_type=F32)


def call(kernel, out_shape, *, grid=(1,), scalars=0, in_specs, out_specs, scratch=(), flops=0, nbytes=0, aliases=None, name=None):
    return pl.pallas_call(
        kernel,
        out_shape=out_shape,
        grid_spec=pltpu.PrefetchScalarGridSpec(
            num_scalar_prefetch=scalars, grid=grid, in_specs=in_specs, out_specs=out_specs, scratch_shapes=scratch
        ),
        compiler_params=pltpu.CompilerParams(vmem_limit_bytes=VMEM_LIMIT),
        cost_estimate=pl.CostEstimate(flops=flops, bytes_accessed=nbytes, transcendentals=0),
        input_output_aliases=aliases or {},
        name=name,
    )


def whole(shape):
    return pl.BlockSpec(shape, lambda *_: (0,) * len(shape))


def rows_at(chunk, width):
    return pl.BlockSpec((chunk, width), lambda s, *_: (s, 0))


def sds(shape, dtype=F32):
    return jax.ShapeDtypeStruct(shape, dtype)


def mask_roots(states, mine, sizes):
    roots, cap, width = states.shape
    chunk = cap // CHUNKS

    def kernel(s_ref, states_ref, own_ref, other_ref):
        row = lax.broadcasted_iota(jnp.int32, (chunk, width), 0) + pl.program_id(0) * chunk
        col = lax.broadcasted_iota(jnp.int32, (chunk, width), 1)
        mask = ((row < s_ref[1]) & (col < s_ref[2])).astype(F32)
        own_ref[...] = states_ref[s_ref[0]] * mask
        other_ref[...] = states_ref[1 - s_ref[0]] * mask

    scal = jnp.stack([mine, sizes[0], sizes[1]])
    return call(
        kernel,
        (sds((cap, width)),) * 2,
        grid=(CHUNKS,),
        scalars=1,
        in_specs=[pl.BlockSpec((roots, chunk, width), lambda s, *_: (0, s, 0))],
        out_specs=(rows_at(chunk, width),) * 2,
        nbytes=4 * states.size * 2,
        name="mask_roots",
    )(scal, states)


def assemble(parts, offsets, forms):
    part_rows, width = parts[0].shape
    total = part_rows * len(parts)

    def kernel(off_ref, *refs):
        parts_in, outs, full = refs[: len(parts)], refs[len(parts) : -1], refs[-1]
        for k, part in enumerate(parts_in):
            full[pl.ds(pl.multiple_of(off_ref[k], 8), part_rows), :] = part[...]
        at = 0
        for form in forms:
            value = full[...] if form == "n" else full[...].T
            hi, lo = split(value)
            outs[at][...] = hi
            outs[at + 1][...] = lo
            at += 2

    outs = []
    for form in forms:
        outs += [sds((total, width) if form == "n" else (width, total), BF16)] * 2
    got = call(
        kernel,
        tuple(outs),
        scalars=1,
        in_specs=[whole((part_rows, width))] * len(parts),
        out_specs=tuple(whole(o.shape) for o in outs),
        scratch=[pltpu.VMEM((total, width), F32)],
        nbytes=8 * total * width,
        name="assemble",
    )(jnp.stack(offsets).astype(jnp.int32), *parts)
    return [tuple(got[2 * k : 2 * k + 2]) for k in range(len(forms))]


def right_products(hop_in, back_in, op):
    cap, width = hop_in.shape
    chunk = cap // CHUNKS

    def kernel(hop_ref, back_ref, rh_ref, rl_ref, th, tl, sh, sl):
        r = (rh_ref[...], rl_ref[...])
        th[...], tl[...] = split(dot_nt(split(hop_ref[...]), r))
        sh[...], sl[...] = split(dot_nn(split(back_ref[...]), r))

    got = call(
        kernel,
        (sds((cap, width), BF16),) * 4,
        grid=(CHUNKS,),
        in_specs=[rows_at(chunk, width)] * 2 + [whole((width, width))] * 2,
        out_specs=(rows_at(chunk, width),) * 4,
        flops=12 * cap * width * width,
        nbytes=4 * cap * width * 5,
        name="right_products",
    )(hop_in, back_in, *op)
    return got[:2], got[2:]


def left_products(hop_op, hop_mid, back_op, back_mid, which, count):
    cap, width = hop_mid[0].shape
    chunk = cap // count

    def kernel(ah, al, th, tl, bh, bl, sh, sl, hop_ref, back_ref):
        hop_ref[...] = dot_nn((ah[...], al[...]), (th[...], tl[...]))
        back_ref[...] = dot_nn((bh[...], bl[...]), (sh[...], sl[...]))

    rows = pl.BlockSpec((chunk, cap), lambda *_: (which, 0))
    full = whole((cap, width))
    return call(
        kernel,
        (sds((chunk, width)),) * 2,
        in_specs=[rows, rows, full, full] * 2,
        out_specs=(whole((chunk, width)),) * 2,
        flops=12 * chunk * cap * width,
        nbytes=4 * cap * width * 3,
        name="left_products",
    )(*hop_op, *hop_mid, *back_op, *back_mid)


def left_local(op, blocks):
    cap, width = blocks[0].shape
    chunk = cap // CHUNKS

    def kernel(lh, ll, m0, m1, o0, o1, keep):
        @pl.when(pl.program_id(0) == 0)
        def _():
            for k, m in enumerate((m0, m1)):
                hi, lo = split(m[...])
                keep[2 * k] = hi
                keep[2 * k + 1] = lo

        a = (lh[...], ll[...])
        o0[...] = dot_nn(a, (keep[0], keep[1]))
        o1[...] = dot_nn(a, (keep[2], keep[3]))

    return call(
        kernel,
        (sds((cap, width)),) * 2,
        grid=(CHUNKS,),
        in_specs=[rows_at(chunk, cap)] * 2 + [whole((cap, width))] * 2,
        out_specs=(rows_at(chunk, width),) * 2,
        scratch=[pltpu.VMEM((4, cap, width), BF16)],
        flops=12 * cap * cap * width,
        nbytes=4 * cap * width * 5,
        name="left_local",
    )(*op, *blocks)


def right_local(op, blocks, sums):
    cap, width = blocks[0].shape
    chunk = cap // CHUNKS

    def kernel(rh, rl, m0, m1, s0, s1, o0, o1):
        r = (rh[...], rl[...])
        o0[...] = s0[...] + dot_nt(split(m0[...]), r)
        o1[...] = s1[...] + dot_nt(split(m1[...]), r)

    return call(
        kernel,
        (sds((cap, width)),) * 2,
        grid=(CHUNKS,),
        in_specs=[whole((width, width))] * 2 + [rows_at(chunk, width)] * 4,
        out_specs=(rows_at(chunk, width),) * 2,
        flops=12 * cap * width * width,
        nbytes=4 * cap * width * 7,
        name="right_local",
    )(*op, *blocks, *sums)


def finish(shape, mine, sizes, own_sum, other_sum, hop, back, returned):
    roots, cap, width = shape
    chunk = cap // len(returned)
    n = len(returned)

    def kernel(s_ref, own_ref, other_ref, hop_ref, back_ref, *refs):
        got, out_ref = refs[:-1], refs[-1]
        step = pl.program_id(0)
        row = lax.broadcasted_iota(jnp.int32, (chunk, width), 0) + step * chunk
        col = lax.broadcasted_iota(jnp.int32, (chunk, width), 1)
        mask = ((row < s_ref[1]) & (col < s_ref[2])).astype(F32)
        out_ref[s_ref[0]] = (own_ref[...] + hop_ref[...] + back_ref[...]) * mask
        for k in range(n):

            @pl.when(step == k)
            def _():
                out_ref[1 - s_ref[0]] = (other_ref[...] + got[k][...]) * mask

    scal = jnp.stack([mine, sizes[0], sizes[1]])
    return call(
        kernel,
        sds(shape),
        grid=(n,),
        scalars=1,
        in_specs=[rows_at(chunk, width)] * 4 + [whole((chunk, width))] * n,
        out_specs=pl.BlockSpec((roots, chunk, width), lambda s, *_: (0, s, 0)),
        nbytes=4 * cap * width * 7,
        name="finish",
    )(scal, own_sum, other_sum, hop, back, *returned)


def on_device(n_l, n_r, states, left_env, right_env, left_op, right_op, sizes_left, sizes_right):
    cap = states.shape[1]
    i, j = lax.axis_index("lsec"), lax.axis_index("rsec")
    mine = (i % 2).astype(jnp.int32)
    sizes = (sizes_left[0], sizes_right[0])

    def move(value, to):
        pairs = []
        for a in range(n_l):
            for b in range(n_r):
                goal = to(a, b)
                if goal is not None and 0 <= goal[0] < n_l and 0 <= goal[1] < n_r:
                    pairs.append((a * n_r + b, goal[0] * n_r + goal[1]))
        return lax.ppermute(value, AXES, pairs)

    swap = lambda v: move(v, lambda a, b: (a ^ 1, b))

    def gathered_left(shard, forms):
        held = {0: shard}
        bit = n_r // 2
        while bit:
            for m in list(held):
                held[m ^ bit] = move(held[m], lambda a, b: (a, b ^ bit))
            bit //= 2
        rows = shard.shape[0]
        keys = list(held)
        return assemble([held[m] for m in keys], [(j ^ m) * rows for m in keys], forms)

    def gathered_right(shard):
        rows = shard.shape[0]
        parts, offsets = [], []
        twin = swap(shard)
        for held, base in ((shard, i), (twin, i ^ 1)):
            for k in range(n_l // 2):
                parts.append(move(held, lambda a, b: ((a + 2 * k) % n_l, b)) if k else held)
                offsets.append(((base - 2 * k) % n_l) * rows)
        return assemble(parts, offsets, "n")[0]

    lo, le = left_op[0], left_env[0]
    ro, re = right_op[0], right_env[0]

    next_lo = move(lo, lambda a, b: (a - 1, b))
    op_r = gathered_right(ro)
    own, other = mask_roots(states, mine, sizes)
    op_l, op_l_t = gathered_left(lo, "nt")
    op_n, op_n_t = gathered_left(next_lo, "nt")
    up = move(own, lambda a, b: (a, b - 1))
    twin = swap(other)

    mid_hop, mid_back = right_products(up, own, op_r)
    returned = []
    for k in range(CHUNKS):
        hop, back = left_products(op_n, mid_hop, op_l_t, mid_back, k, CHUNKS)
        hop_far = move(hop, lambda a, b: (a + 2, b) if a % 2 else None)
        back_far = move(back, lambda a, b: (a if a % 2 else a - 2, b + 1))
        returned.append(swap(jnp.where(mine == 0, hop, hop_far) + back_far))

    env_l = gathered_left(le, "n")[0]
    sums = left_local(env_l, (own, other))
    twin_hop = move(twin, lambda a, b: (a if a % 2 else a + 2, b - 1))
    twin_next = move(twin, lambda a, b: (a - 2, b) if a % 2 else None)
    twin_back = jnp.where(mine == 0, twin, twin_next)
    mid_hop2, mid_back2 = right_products(twin_hop, twin_back, op_r)
    hop2, back2 = left_products(op_l, mid_hop2, op_n_t, mid_back2, 0, 1)
    back2 = move(back2, lambda a, b: (a, b + 1))
    env_r = gathered_right(re)
    own_sum, other_sum = right_local(env_r, (own, other), sums)
    return finish(states.shape, mine, sizes, own_sum, other_sum, hop2, back2, returned)


def solution(mesh):
    in_specs = (
        P(None, "lsec", "rsec"),
        P("lsec", "rsec", None),
        P("rsec", "lsec", None),
        P("lsec", "rsec", None),
        P("rsec", "lsec", None),
        P("lsec"),
        P("rsec"),
    )
    body = functools.partial(on_device, mesh.shape["lsec"], mesh.shape["rsec"])
    return jax.shard_map(
        body, mesh=mesh, in_specs=in_specs, out_specs=P(None, "lsec", "rsec"), check_vma=False
    )
```

```python
import jax
import jax.numpy as jnp
from jax import lax
from jax.experimental import pallas as pl
from jax.experimental.pallas import tpu as pltpu
from jax.sharding import PartitionSpec as P

AXES = ("lsec", "rsec")
CHUNKS = 4
PARTS = 2
RETURNS = 2
F32, BF16 = jnp.float32, jnp.bfloat16
MIB = 1024 * 1024


def split(x):
    hi = x.astype(BF16)
    return hi, (x - hi.astype(F32)).astype(BF16)


def dot_nn(a, b):
    left = jnp.concatenate([a[0], a[0], a[1]], axis=1)
    right = jnp.concatenate([b[0], b[1], b[0]], axis=0)
    return lax.dot_general(left, right, (((1,), (0,)), ((), ())), preferred_element_type=F32)


def dot_nt(a, b):
    left = jnp.concatenate([a[0], a[0], a[1]], axis=1)
    right = jnp.concatenate([b[0], b[1], b[0]], axis=1)
    return lax.dot_general(left, right, (((1,), (1,)), ((), ())), preferred_element_type=F32)


def call(kernel, out_shape, *, grid=(1,), scalars=0, in_specs, out_specs, scratch=(), flops=0, nbytes=0, aliases=None, mib=12):
    return pl.pallas_call(
        kernel,
        out_shape=out_shape,
        grid_spec=pltpu.PrefetchScalarGridSpec(
            num_scalar_prefetch=scalars, grid=grid, in_specs=in_specs, out_specs=out_specs, scratch_shapes=scratch
        ),
        compiler_params=pltpu.CompilerParams(vmem_limit_bytes=mib * MIB),
        cost_estimate=pl.CostEstimate(flops=flops, bytes_accessed=nbytes, transcendentals=0),
        input_output_aliases=aliases or {},
    )


def whole(shape):
    return pl.BlockSpec(shape, lambda *_: (0,) * len(shape))


def rows_at(chunk, width):
    return pl.BlockSpec((chunk, width), lambda s, *_: (s, 0))


def sds(shape, dtype=F32):
    return jax.ShapeDtypeStruct(shape, dtype)


def mask_roots(states, mine, sizes):
    roots, cap, width = states.shape
    chunk = cap // CHUNKS
    per = CHUNKS // PARTS

    def kernel(s_ref, states_ref, own_ref, *other_refs):
        step = pl.program_id(0)
        row = lax.broadcasted_iota(jnp.int32, (chunk, width), 0) + step * chunk
        col = lax.broadcasted_iota(jnp.int32, (chunk, width), 1)
        keep = (row < s_ref[1]) & (col < s_ref[2])
        own_ref[...] = jnp.where(keep, states_ref[s_ref[0]], 0.0)
        for k, ref in enumerate(other_refs):

            @pl.when(step // per == k)
            def _():
                ref[...] = jnp.where(keep, states_ref[1 - s_ref[0]], 0.0)

    scal = jnp.stack([mine, sizes[0], sizes[1]])
    piece = [pl.BlockSpec((chunk, width), lambda s, *_, k=k: (jnp.clip(s - k * per, 0, per - 1), 0)) for k in range(PARTS)]
    own, *other = call(
        kernel,
        (sds((cap, width)),) + (sds((cap // PARTS, width)),) * PARTS,
        grid=(CHUNKS,),
        scalars=1,
        in_specs=[pl.BlockSpec((roots, chunk, width), lambda s, *_: (0, s, 0))],
        out_specs=(rows_at(chunk, width), *piece),
        nbytes=4 * states.size * 2,
    )(scal, states)
    return own, other


def assemble(parts, offsets, forms):
    unit = parts[0].shape[0] * len(parts) // len(offsets)
    width = parts[0].shape[1]
    total = unit * len(offsets)

    def kernel(off_ref, *refs):
        parts_in, outs, full = refs[: len(parts)], refs[len(parts) : -1], refs[-1]
        at = 0
        for part in parts_in:
            for sub in range(part.shape[0] // unit):
                full[pl.ds(pl.multiple_of(off_ref[at], 8), unit), :] = part[pl.ds(sub * unit, unit), :]
                at += 1
        at = 0
        for form in forms:
            if form == "f":
                outs[at][...] = full[...]
                at += 1
                continue
            hi, lo = split(full[...] if form == "n" else full[...].T)
            outs[at][...] = hi
            outs[at + 1][...] = lo
            at += 2

    outs, spans = [], []
    for form in forms:
        shape = (width, total) if form == "t" else (total, width)
        new = [sds(shape)] if form == "f" else [sds(shape, BF16)] * 2
        spans.append((len(outs), len(outs) + len(new)))
        outs += new
    got = call(
        kernel,
        tuple(outs),
        scalars=1,
        in_specs=[whole(p.shape) for p in parts],
        out_specs=tuple(whole(o.shape) for o in outs),
        scratch=[pltpu.VMEM((total, width), F32)],
        nbytes=8 * total * width,
    )(jnp.stack(offsets).astype(jnp.int32), *parts)
    return [got[x] if y - x == 1 else tuple(got[x:y]) for x, y in spans]


def fetched(kernel, inputs, in_scratch, outs, out_scratch, *, scalars=None, extra=(), aliases=None, flops, mib):
    n_in, n_out = len(inputs), len(outs)
    n_s = 0 if scalars is None else 1

    def body(*refs):
        s_ref, refs = refs[:n_s], refs[n_s:]
        ins, out_refs, refs = refs[:n_in], refs[n_in : n_in + n_out], refs[n_in + n_out :]
        bufs, refs = refs[: len(in_scratch)], refs[len(in_scratch) :]
        results, refs = refs[: len(out_scratch)], refs[len(out_scratch) :]
        sems, rest = refs[0], refs[1:]
        groups, sem = [], 0
        for buf, (_, _, sources) in zip(bufs, in_scratch):
            group, at = [], 0
            for src in sources:
                rows = inputs[src].shape[0]
                group.append(pltpu.make_async_copy(ins[src], buf.at[pl.ds(at, rows)], sems.at[sem]))
                at, sem = at + rows, sem + 1
            groups.append(group)
            for copy in group:
                copy.start()
        sent = []

        def get(k):
            for copy in groups[k]:
                copy.wait()
            return bufs[k][...]

        def put(k, value, to=None):
            nonlocal sem
            results[k][...] = value
            at = 0
            for dst in out_scratch[k][1]:
                ref = out_refs[dst] if to is None else to(out_refs[dst])
                rows = ref.shape[0]
                copy = pltpu.make_async_copy(results[k].at[pl.ds(at, rows)], ref, sems.at[sem])
                copy.start()
                sent.append(copy)
                at, sem = at + rows, sem + 1

        kernel(get, put, s_ref[0] if n_s else None, rest)
        for copy in sent:
            copy.wait()

    n_sem = sum(len(x[2]) for x in in_scratch) + sum(len(x[1]) for x in out_scratch)
    scratch = [pltpu.VMEM(shape, dtype) for shape, dtype, _ in in_scratch]
    scratch += [pltpu.VMEM(shape, F32) for shape, _ in out_scratch]
    scratch += [pltpu.SemaphoreType.DMA((n_sem,)), *extra]
    anywhere = pl.BlockSpec(memory_space=pl.ANY)
    return call(
        body,
        tuple(outs),
        scalars=n_s,
        in_specs=[anywhere] * n_in,
        out_specs=(anywhere,) * n_out,
        scratch=scratch,
        flops=flops,
        nbytes=sum(x.size * 4 for x in inputs),
        aliases=aliases,
        mib=mib,
    )(*(() if scalars is None else (scalars,)), *inputs)


def hub_out(up, own, op_r, op_n, op_l_t):
    cap, width = own.shape
    square, chunk = (width, width), sds((cap // RETURNS, width))

    def kernel(get, put, _, rest):
        (mid,) = rest
        r = split(get(0))
        mid[0], mid[1] = split(dot_nt(split(get(1)), r))
        mid[2], mid[3] = split(dot_nn(split(get(2)), r))
        put(0, dot_nn((get(3), get(4)), (mid[0], mid[1])))
        put(1, dot_nn((get(5), get(6)), (mid[2], mid[3])))

    blocks = [(square, F32, [0])] + [((cap, width), F32, [k]) for k in (1, 2)]
    blocks += [((cap, cap), BF16, [k]) for k in (3, 4, 5, 6)]
    got = fetched(
        kernel,
        [op_r, up, own, *op_n, *op_l_t],
        blocks,
        [chunk] * (2 * RETURNS),
        [((cap, width), list(range(RETURNS))), ((cap, width), list(range(RETURNS, 2 * RETURNS)))],
        extra=[pltpu.VMEM((4, cap, width), BF16)],
        flops=24 * cap * cap * width,
        mib=30,
    )
    return got[:RETURNS], got[RETURNS:]


def hub_own(shape, scal, hop_in, back_in, op_r, op_prev, op_l, op_n_t, own_sum):
    _, cap, width = shape
    square, n = (width, width), len(hop_in)

    def kernel(get, put, s_ref, rest):
        (mid,) = rest
        mid[0], mid[1] = split(dot_nt(split(get(1)), split(get(0))))
        mid[2], mid[3] = split(dot_nn(split(get(3)), split(get(2))))
        total = get(8) + dot_nn((get(4), get(5)), (mid[0], mid[1])) + dot_nn((get(6), get(7)), (mid[2], mid[3]))
        row = lax.broadcasted_iota(jnp.int32, (cap, width), 0)
        col = lax.broadcasted_iota(jnp.int32, (cap, width), 1)
        total = jnp.where((row < s_ref[1]) & (col < s_ref[2]), total, 0.0)
        put(0, total, lambda ref: ref.at[s_ref[0]])

    inputs = [op_r, *hop_in, op_prev, *back_in, *op_l, *op_n_t, own_sum]
    place = [[0], list(range(1, n + 1)), [n + 1], list(range(n + 2, 2 * n + 2))] + [[2 * n + 2 + k] for k in range(5)]
    kinds = [(square, F32), ((cap, width), F32)] * 2 + [((cap, cap), BF16)] * 4 + [((cap, width), F32)]
    return fetched(
        kernel,
        inputs,
        [(*kind, where) for kind, where in zip(kinds, place)],
        [sds(shape)],
        [((cap, width), [0])],
        scalars=scal,
        extra=[pltpu.VMEM((4, cap, width), BF16)],
        flops=24 * cap * cap * width,
        mib=30,
    )[0]


def left_local(op, own, other):
    cap, width = own.shape
    n = len(other)

    def kernel(get, put, _, rest):
        a = (get(0), get(1))
        put(0, dot_nn(a, split(get(2))))
        put(1, dot_nn(a, split(get(3))))

    return fetched(
        kernel,
        [*op, own, *other],
        [((cap, cap), BF16, [0]), ((cap, cap), BF16, [1]), ((cap, width), F32, [2]), ((cap, width), F32, list(range(3, 3 + n)))],
        [sds((cap, width))] * 2,
        [((cap, width), [k]) for k in range(2)],
        flops=12 * cap * cap * width,
        mib=24,
    )


def right_local(op, own, other, sums):
    cap, width = own.shape
    n = len(other)

    def kernel(get, put, _, rest):
        r = (get(0), get(1))
        value = dot_nt(split(get(2)), r)
        put(0, get(4) + value)
        value = dot_nt(split(get(3)), r)
        put(1, get(5) + value)

    full = (cap, width)
    return fetched(
        kernel,
        [*op, own, *other, *sums],
        [((width, width), BF16, [0]), ((width, width), BF16, [1]), (full, F32, [2]), (full, F32, list(range(3, 3 + n)))]
        + [(full, F32, [3 + n + k]) for k in range(2)],
        [sds(full)] * 2,
        [(full, [k]) for k in range(2)],
        flops=12 * cap * width * width,
        mib=24,
    )


def combine(mine, hop, hop_far, back_far):
    def kernel(s_ref, a, b, c, out):
        out[...] = jnp.where(s_ref[0] == 0, a[...], b[...]) + c[...]

    return call(
        kernel,
        sds(hop.shape),
        scalars=1,
        in_specs=[whole(hop.shape)] * 3,
        out_specs=whole(hop.shape),
        nbytes=16 * hop.size,
    )(mine[None], hop, hop_far, back_far)


def finish(partial, scal, other_sum, returned):
    _, cap, width = partial.shape
    n = len(returned)
    chunk = cap // n

    def kernel(s_ref, _, other_ref, *refs):
        got, out_ref = refs[:-1], refs[-1]
        step = pl.program_id(0)
        row = lax.broadcasted_iota(jnp.int32, (chunk, width), 0) + step * chunk
        col = lax.broadcasted_iota(jnp.int32, (chunk, width), 1)
        keep = (row < s_ref[1]) & (col < s_ref[2])
        for k in range(n):

            @pl.when(step == k)
            def _():
                out_ref[0] = jnp.where(keep, other_ref[...] + got[k][...], 0.0)

    return call(
        kernel,
        sds(partial.shape),
        grid=(n,),
        scalars=1,
        in_specs=[pl.BlockSpec(memory_space=pl.ANY), rows_at(chunk, width)] + [whole((chunk, width))] * n,
        out_specs=pl.BlockSpec((1, chunk, width), lambda s, s_ref: (1 - s_ref[0], s, 0)),
        nbytes=4 * cap * width * 3,
        aliases={1: 0},
    )(scal, partial, other_sum, *returned)


def on_device(n_l, n_r, states, left_env, right_env, left_op, right_op, sizes_left, sizes_right):
    i, j = lax.axis_index("lsec"), lax.axis_index("rsec")
    mine = (i % 2).astype(jnp.int32)
    sizes = (sizes_left[0], sizes_right[0])

    def move(value, to):
        pairs = []
        for a in range(n_l):
            for b in range(n_r):
                goal = to(a, b)
                if goal is not None and 0 <= goal[0] < n_l and 0 <= goal[1] < n_r:
                    pairs.append((a * n_r + b, goal[0] * n_r + goal[1]))
        return lax.ppermute(value, AXES, pairs)

    def swap(value):
        return move(value, lambda a, b: (a ^ 1, b))

    def spread_left(shard):
        held = {0: shard}
        bit = n_r // 2
        while bit:
            for m in list(held):
                held[m ^ bit] = move(held[m], lambda a, b: (a, b ^ bit))
            bit //= 2
        return held

    def spread_right(shard):
        return [shard] + [move(shard, lambda a, b: ((a + 2 * k) % n_l, b)) for k in range(1, n_l // 2)]

    lo, le = left_op[0], left_env[0]
    ro, re = right_op[0], right_env[0]
    rows_l, rows_r = lo.shape[0], ro.shape[0]

    def right_offsets(base):
        return [((base - 2 * k) % n_l) * rows_r for k in range(n_l // 2)]

    twin_ro = swap(ro)
    all_lo = spread_left(lo)
    next_lo = move(lo, lambda a, b: (a - 1, b))
    all_le = spread_left(le)
    own, other = mask_roots(states, mine, sizes)
    all_r = spread_right(ro) + spread_right(twin_ro)
    half_re = spread_right(re)
    twin = [swap(piece) for piece in other]
    all_n = spread_left(next_lo)
    up = move(own, lambda a, b: (a, b - 1))
    keys = list(all_lo)
    at = [(j ^ m) * rows_l for m in keys]
    (env_l,) = assemble([all_le[m] for m in keys], at, "n")
    sums = left_local(env_l, own, other)
    op_l, op_l_t = assemble([all_lo[m] for m in keys], at, "nt")
    op_n, op_n_t = assemble([all_n[m] for m in keys], at, "nt")
    twin_hop = [move(v, lambda a, b: (a if a % 2 else a + 2, b - 1)) for v in twin]
    twin_next = [move(v, lambda a, b: (a - 2 if a % 2 else a, b + 1)) for v in twin]
    (op_r,) = assemble(all_r, right_offsets(i) + right_offsets(i ^ 1), "f")
    op_prev = move(op_r, lambda a, b: (a, b + 1))

    hops, backs = hub_out(up, own, op_r, op_n, op_l_t)
    returned = []
    for hop, back in zip(hops, backs):
        hop_far = move(hop, lambda a, b: (a + 2, b) if a % 2 else None)
        back_far = move(back, lambda a, b: (a if a % 2 else a - 2, b + 1))
        returned.append(swap(combine(mine, hop, hop_far, back_far)))

    own_places = right_offsets(i) + right_offsets(i ^ 1)
    (half,) = assemble(half_re, [jnp.int32(k * rows_r) for k in range(n_l // 2)], "f")
    (env_r,) = assemble([half, swap(half)], own_places, "n")
    own_sum, other_sum = right_local(env_r, own, other, sums)
    scal = jnp.stack([mine, *sizes])
    partial = hub_own(states.shape, scal, twin_hop, twin_next, op_r, op_prev, op_l, op_n_t, own_sum)
    return finish(partial, scal, other_sum, returned)


def solution(mesh):
    in_specs = (
        P(None, "lsec", "rsec"),
        P("lsec", "rsec", None),
        P("rsec", "lsec", None),
        P("lsec", "rsec", None),
        P("rsec", "lsec", None),
        P("lsec"),
        P("rsec"),
    )
    n_l, n_r = mesh.shape["lsec"], mesh.shape["rsec"]

    def body(*args):
        return on_device(n_l, n_r, *args)

    return jax.shard_map(
        body, mesh=mesh, in_specs=in_specs, out_specs=P(None, "lsec", "rsec"), check_vma=False
    )
```

```python
import jax
import jax.numpy as jnp
from jax import lax
from jax.experimental import pallas as pl
from jax.experimental.pallas import tpu as pltpu
from jax.sharding import PartitionSpec as P

AXES = ("lsec", "rsec")
RETURNS = (2, 2, 1)
TWIN = (2, 3)
F32, BF16 = jnp.float32, jnp.bfloat16
MIB = 1024 * 1024


def split(x):
    hi = x.astype(BF16)
    return hi, (x - hi.astype(F32)).astype(BF16)


def dot_nn(a, b):
    left = jnp.concatenate([a[0], a[0], a[1]], axis=1)
    right = jnp.concatenate([b[0], b[1], b[0]], axis=0)
    return lax.dot_general(left, right, (((1,), (0,)), ((), ())), preferred_element_type=F32)


def dot_nt(a, b):
    left = jnp.concatenate([a[0], a[0], a[1]], axis=1)
    right = jnp.concatenate([b[0], b[1], b[0]], axis=1)
    return lax.dot_general(left, right, (((1,), (1,)), ((), ())), preferred_element_type=F32)


def call(kernel, out_shape, *, grid=(1,), scalars=0, in_specs, out_specs, scratch=(), flops=0, nbytes=0, aliases=None, mib=12):
    return pl.pallas_call(
        kernel,
        out_shape=out_shape,
        grid_spec=pltpu.PrefetchScalarGridSpec(
            num_scalar_prefetch=scalars, grid=grid, in_specs=in_specs, out_specs=out_specs, scratch_shapes=scratch
        ),
        compiler_params=pltpu.CompilerParams(vmem_limit_bytes=mib * MIB),
        cost_estimate=pl.CostEstimate(flops=flops, bytes_accessed=nbytes, transcendentals=0),
        input_output_aliases=aliases or {},
    )


def whole(shape):
    return pl.BlockSpec(shape, lambda *_: (0,) * len(shape))


def rows_at(chunk, width):
    return pl.BlockSpec((chunk, width), lambda s, *_: (s, 0))


def sds(shape, dtype=F32):
    return jax.ShapeDtypeStruct(shape, dtype)


def mask_roots(states, scal, pieces):
    roots, cap, width = states.shape
    step = cap // sum(TWIN)

    def kernel(s_ref, states_ref, own_ref, own_hi, own_lo, other_hi, other_lo, *other_refs):
        row = lax.broadcasted_iota(jnp.int32, (step, width), 0) + pl.program_id(0) * step
        col = lax.broadcasted_iota(jnp.int32, (step, width), 1)
        keep = (row < s_ref[1]) & (col < s_ref[2])
        own = jnp.where(keep, states_ref[s_ref[0]], 0.0)
        own_ref[...] = own
        own_hi[...], own_lo[...] = split(own)
        other = jnp.where(keep, states_ref[1 - s_ref[0]], 0.0)
        other_hi[...], other_lo[...] = split(other)
        first = 0
        for part, ref in zip(TWIN, other_refs):

            @pl.when((pl.program_id(0) >= first) & (pl.program_id(0) < first + part))
            def _():
                ref[...] = other

            first += part

    piece_specs, first = [], 0
    for part in TWIN:
        piece_specs.append(pl.BlockSpec((step, width), lambda s, *_, first=first, part=part: (jnp.clip(s - first, 0, part - 1), 0)))
        first += part
    half = sds((cap, width), BF16)
    own, own_hi, own_lo, other_hi, other_lo, *others = call(
        kernel,
        (sds((cap, width)), half, half, half, half) + tuple(sds((rows, width)) for rows in pieces),
        grid=(sum(TWIN),),
        scalars=1,
        in_specs=[pl.BlockSpec((roots, step, width), lambda s, *_: (0, s, 0))],
        out_specs=(rows_at(step, width),) * 5 + tuple(piece_specs),
        nbytes=4 * states.size * 3,
    )(scal, states)
    return own, (own_hi, own_lo), others, (other_hi, other_lo)


def fetched(kernel, inputs, buffers, outs, results, *, scalars, root=None, passed=(), extra=(), aliases=None, flops=0, mib):
    n_in, n_out = len(inputs), len(outs)
    laid = [k for k, (_, fills) in enumerate(buffers) if len(fills) > 1]
    direct = {k for k, _ in passed}

    def body(s_ref, *refs):
        ins, out_refs, refs = refs[:n_in], refs[n_in : n_in + n_out], refs[n_in + n_out :]
        bufs = dict(zip([k for k in laid if k not in direct], refs))
        rest = refs[len(bufs) :]
        for k, dst in passed:
            bufs[k] = out_refs[dst]

        def lay(k):
            for src, first, rows, to in buffers[k][1]:
                to = pl.multiple_of(to(s_ref), 8) if callable(to) else to
                bufs[k][pl.ds(to, rows), :] = ins[src][pl.ds(first, rows), :]

        def get(k):
            if k not in bufs:
                return ins[buffers[k][1][0][0]][...]
            lay(k)
            return bufs[k][...]

        def put(k, value):
            at = 0
            for dst in results[k][1]:
                rows = outs[dst].shape[-2]
                if root is None:
                    out_refs[dst][...] = value[at : at + rows]
                else:
                    out_refs[dst][0] = value
                at += rows

        def pass_on():
            for k, _ in passed:
                lay(k)

        kernel(get, put, pass_on, s_ref, *rest)

    scratch = [pltpu.VMEM(buffers[k][0], inputs[buffers[k][1][0][0]].dtype) for k in laid if k not in direct]
    used = {fill[0] for _, fills in buffers for fill in fills}
    in_specs = [whole(x.shape) if k in used else pl.BlockSpec(memory_space=pl.ANY) for k, x in enumerate(inputs)]
    if root is None:
        out_specs = tuple(whole(x.shape) for x in outs)
    else:
        out_specs = tuple(pl.BlockSpec((1, *x.shape[1:]), lambda s, s_ref: (root(s_ref), 0, 0)) for x in outs)
    return call(
        body,
        tuple(outs),
        scalars=1,
        in_specs=in_specs,
        out_specs=out_specs,
        scratch=scratch + list(extra),
        flops=flops,
        nbytes=sum(x.size * 4 for x in (*inputs, *outs)),
        aliases=aliases,
        mib=mib,
    )(scalars, *inputs)


class Operands:
    def __init__(self):
        self.inputs = []

    def add(self, array):
        for k, known in enumerate(self.inputs):
            if known is array:
                return k
        self.inputs.append(array)
        return len(self.inputs) - 1

    def stacked(self, *arrays):
        fills, at = [], 0
        for array in arrays:
            fills.append((self.add(array), 0, array.shape[0], at))
            at += array.shape[0]
        return (at, arrays[0].shape[1]), fills

    def placed(self, arrays, unit, first_scalar):
        fills = []
        for array in arrays:
            for sub in range(array.shape[0] // unit):
                at = first_scalar + len(fills)
                fills.append((self.add(array), sub * unit, unit, lambda s_ref, at=at: s_ref[at]))
        return (unit * len(fills), arrays[0].shape[1]), fills


def masked(value, s_ref):
    row = lax.broadcasted_iota(jnp.int32, value.shape, 0)
    col = lax.broadcasted_iota(jnp.int32, value.shape, 1)
    return jnp.where((row < s_ref[1]) & (col < s_ref[2]), value, 0.0)


def hub_out(scal, at_l, pieces, up, own, op_r, next_parts, lo_parts):
    cap, width = up.shape
    n = len(pieces)
    ops = Operands()
    buffers = [
        ops.stacked(op_r),
        ops.stacked(own[0]),
        ops.stacked(own[1]),
        ops.placed(lo_parts, lo_parts[0].shape[0], at_l),
        ops.stacked(up),
        ops.placed(next_parts, next_parts[0].shape[0], at_l),
    ]

    def kernel(get, put, pass_on, s_ref, mid):
        r = split(get(0))
        mid[0], mid[1] = split(dot_nn((get(1), get(2)), r))
        put(0, dot_nn(split(get(3).T), (mid[0], mid[1])))
        mid[2], mid[3] = split(dot_nt(split(get(4)), r))
        put(1, dot_nn(split(get(5)), (mid[2], mid[3])))

    got = fetched(
        kernel,
        ops.inputs,
        buffers,
        [sds((rows, width)) for rows in pieces] * 2,
        [((cap, width), list(range(n))), ((cap, width), list(range(n, 2 * n)))],
        scalars=scal,
        extra=[pltpu.VMEM((4, cap, width), BF16)],
        flops=24 * cap * cap * width,
        mib=30,
    )
    return got[n:], got[:n]


def joined(scal, parts, at=None, unit=None):
    ops = Operands()
    buffers = [ops.stacked(*parts) if at is None else ops.placed(parts, unit, at)]
    return fetched(
        lambda get, put, pass_on, s_ref: pass_on(),
        ops.inputs,
        buffers,
        [sds(buffers[0][0])],
        [],
        scalars=scal,
        passed=[(0, 0)],
        mib=8,
    )[0]


def right_product(scal, piece, op_r):
    ops = Operands()
    buffers = [ops.stacked(op_r), ops.stacked(piece)]

    def kernel(get, put, pass_on, s_ref):
        put(0, dot_nn(split(get(1)), split(get(0))))

    return fetched(
        kernel,
        ops.inputs,
        buffers,
        [sds(piece.shape)],
        [(piece.shape, [0])],
        scalars=scal,
        flops=6 * piece.size * piece.shape[1],
        mib=16,
    )[0]


def hub_own(scal, at_l, shape, hop_in, back_mid, op_r, lo_parts, next_parts, own_sum):
    _, cap, width = shape
    ops = Operands()
    buffers = [
        ops.stacked(op_r),
        ops.stacked(*hop_in),
        ops.stacked(*back_mid),
        ops.placed(lo_parts, lo_parts[0].shape[0], at_l),
        ops.placed(next_parts, next_parts[0].shape[0], at_l),
        ops.stacked(own_sum),
    ]

    def kernel(get, put, pass_on, s_ref, mid):
        mid[0], mid[1] = split(dot_nt(split(get(1)), split(get(0))))
        total = dot_nn(split(get(4).T), split(get(2))) + get(5)
        total = total + dot_nn(split(get(3)), (mid[0], mid[1]))
        put(0, masked(total, s_ref))

    return fetched(
        kernel,
        ops.inputs,
        buffers,
        [sds(shape)],
        [((cap, width), [0])],
        scalars=scal,
        root=lambda s_ref: s_ref[0],
        extra=[pltpu.VMEM((2, cap, width), BF16)],
        flops=18 * cap * cap * width,
        mib=30,
    )[0]


def left_local(scal, at_l, le_parts, own, other):
    cap, width = own[0].shape
    ops = Operands()
    buffers = [ops.placed(le_parts, le_parts[0].shape[0], at_l)] + [ops.stacked(x) for x in (*own, *other)]

    def kernel(get, put, pass_on, s_ref):
        a = split(get(0))
        put(0, dot_nn(a, (get(1), get(2))))
        put(1, dot_nn(a, (get(3), get(4))))

    return fetched(
        kernel,
        ops.inputs,
        buffers,
        [sds((cap, width))] * 2,
        [((cap, width), [k]) for k in range(2)],
        scalars=scal,
        flops=12 * cap * cap * width,
        mib=24,
    )


def right_local(scal, at_r, halves, unit, own, other, sums):
    cap, width = own[0].shape
    ops = Operands()
    buffers = [ops.placed(halves, unit, at_r)] + [ops.stacked(x) for x in (*own, *other, *sums)]

    def kernel(get, put, pass_on, s_ref):
        r = split(get(0))
        value = dot_nt((get(1), get(2)), r)
        put(0, get(5) + value)
        value = dot_nt((get(3), get(4)), r)
        put(1, get(6) + value)

    return fetched(
        kernel,
        ops.inputs,
        buffers,
        [sds((cap, width))] * 2,
        [((cap, width), [k]) for k in range(2)],
        scalars=scal,
        flops=12 * cap * width * width,
        mib=26,
    )


def combine(mine, hop, hop_far, back_far):
    def kernel(s_ref, a, b, c, out):
        out[...] = jnp.where(s_ref[0] == 0, a[...], b[...]) + c[...]

    return call(
        kernel,
        sds(hop.shape),
        scalars=1,
        in_specs=[whole(hop.shape)] * 3,
        out_specs=whole(hop.shape),
        nbytes=16 * hop.size,
    )(mine[None], hop, hop_far, back_far)


def finish(partial, scal, other_sum, returned):
    ops = Operands()
    buffers = [ops.stacked(other_sum), ops.stacked(*returned)]
    place = ops.add(partial)

    def kernel(get, put, pass_on, s_ref):
        total = get(0)
        put(0, masked(total + get(1), s_ref))

    return fetched(
        kernel,
        ops.inputs,
        buffers,
        [sds(partial.shape)],
        [(other_sum.shape, [0])],
        scalars=scal,
        root=lambda s_ref: 1 - s_ref[0],
        aliases={1 + place: 0},
        mib=12,
    )[0]


def on_device(n_l, n_r, states, left_env, right_env, left_op, right_op, sizes_left, sizes_right):
    cap = states.shape[1]
    i, j = lax.axis_index("lsec"), lax.axis_index("rsec")
    mine = (i % 2).astype(jnp.int32)
    sizes = (sizes_left[0], sizes_right[0])

    def move(value, to):
        pairs = []
        for a in range(n_l):
            for b in range(n_r):
                goal = to(a, b)
                if goal is not None and 0 <= goal[0] < n_l and 0 <= goal[1] < n_r:
                    pairs.append((a * n_r + b, goal[0] * n_r + goal[1]))
        return lax.ppermute(value, AXES, pairs)

    def swap(value):
        return move(value, lambda a, b: (a ^ 1, b))

    def spread_left(shard):
        held = {0: shard}
        bit = n_r // 2
        while bit:
            for m in list(held):
                held[m ^ bit] = move(held[m], lambda a, b: (a, b ^ bit))
            bit //= 2
        return held

    def spread_right(shard):
        return [shard] + [move(shard, lambda a, b: ((a + 2 * k) % n_l, b)) for k in range(1, n_l // 2)]

    lo, le = left_op[0], left_env[0]
    ro, re = right_op[0], right_env[0]
    rows_l, rows_r = lo.shape[0], ro.shape[0]

    def right_rows(base):
        return [((base - 2 * k) % n_l) * rows_r for k in range(n_l // 2)]

    next_lo = move(lo, lambda a, b: (a - 1, b))
    all_lo, all_le, all_n = spread_left(lo), spread_left(le), spread_left(next_lo)
    keys = list(all_lo)
    all_lo, all_le, all_n = ([held[m] for m in keys] for held in (all_lo, all_le, all_n))
    left_rows = [(j ^ m) * rows_l for m in keys]
    own_rows, twin_rows = right_rows(i), right_rows(i ^ 1)
    paired = [row for pair in zip(own_rows, twin_rows) for row in pair]
    scal = jnp.stack([mine, *sizes, *left_rows, *own_rows, *twin_rows, *paired]).astype(jnp.int32)
    at_l, at_r, at_e = 3, 3 + n_r, 3 + n_r + n_l

    twin_pieces = [cap * part // sum(TWIN) for part in TWIN]
    own, own_split, other, other_split = mask_roots(states, scal, twin_pieces)
    twin = [swap(piece) for piece in other]
    half_r = joined(scal, spread_right(ro))
    all_e = spread_right(joined(scal, [re, swap(re)]))
    up = move(own, lambda a, b: (a, b - 1))
    op_r = joined(scal, [half_r, swap(half_r)], at_r, rows_r)
    twin_hop = [move(v, lambda a, b: (a if a % 2 else a + 2, b - 1)) for v in twin]
    twin_mid = [right_product(scal, v, op_r) for v in twin]
    twin_mid = [move(v, lambda a, b: (a - 2 if a % 2 else a, b + 1)) for v in twin_mid]

    pieces = [cap * part // sum(RETURNS) for part in RETURNS]
    hops, backs = hub_out(scal, at_l, pieces, up, own_split, op_r, all_n, all_lo)
    returned = []
    for hop, back in zip(hops, backs):
        hop_far = move(hop, lambda a, b: (a + 2, b) if a % 2 else None)
        back_far = move(back, lambda a, b: (a if a % 2 else a - 2, b + 1))
        returned.append(swap(combine(mine, hop, hop_far, back_far)))

    sums = left_local(scal, at_l, all_le, own_split, other_split)
    own_sum, other_sum = right_local(scal, at_e, all_e, rows_r, own_split, other_split, sums)
    partial = hub_own(scal, at_l, states.shape, twin_hop, twin_mid, op_r, all_lo, all_n, own_sum)
    return finish(partial, scal, other_sum, returned)


def solution(mesh):
    in_specs = (
        P(None, "lsec", "rsec"),
        P("lsec", "rsec", None),
        P("rsec", "lsec", None),
        P("lsec", "rsec", None),
        P("rsec", "lsec", None),
        P("lsec"),
        P("rsec"),
    )
    n_l, n_r = mesh.shape["lsec"], mesh.shape["rsec"]

    def body(*args):
        return on_device(n_l, n_r, *args)

    return jax.shard_map(
        body, mesh=mesh, in_specs=in_specs, out_specs=P(None, "lsec", "rsec"), check_vma=False
    )
```

```python
import jax
import jax.numpy as jnp
from jax import lax
from jax.experimental import pallas as pl
from jax.experimental.pallas import tpu as pltpu
from jax.sharding import PartitionSpec as P

AXES = ("lsec", "rsec")
RETURNS = (2, 2, 1)
TWIN = (2, 3)
F32, BF16 = jnp.float32, jnp.bfloat16
MIB = 1024 * 1024


def split(x):
    hi = x.astype(BF16)
    return hi, (x - hi.astype(F32)).astype(BF16)


def dot_nn(a, b):
    left = jnp.concatenate([a[0], a[0], a[1]], axis=1)
    right = jnp.concatenate([b[0], b[1], b[0]], axis=0)
    return lax.dot_general(left, right, (((1,), (0,)), ((), ())), preferred_element_type=F32)


def dot_nt(a, b):
    left = jnp.concatenate([a[0], a[0], a[1]], axis=1)
    right = jnp.concatenate([b[0], b[1], b[0]], axis=1)
    return lax.dot_general(left, right, (((1,), (1,)), ((), ())), preferred_element_type=F32)


def call(kernel, out_shape, *, grid=(1,), scalars=0, in_specs, out_specs, scratch=(), flops=0, nbytes=0, aliases=None, mib=12):
    return pl.pallas_call(
        kernel,
        out_shape=out_shape,
        grid_spec=pltpu.PrefetchScalarGridSpec(
            num_scalar_prefetch=scalars, grid=grid, in_specs=in_specs, out_specs=out_specs, scratch_shapes=scratch
        ),
        compiler_params=pltpu.CompilerParams(vmem_limit_bytes=mib * MIB),
        cost_estimate=pl.CostEstimate(flops=flops, bytes_accessed=nbytes, transcendentals=0),
        input_output_aliases=aliases or {},
    )


def whole(shape):
    return pl.BlockSpec(shape, lambda *_: (0,) * len(shape))


def rows_at(chunk, width):
    return pl.BlockSpec((chunk, width), lambda s, *_: (s, 0))


def sds(shape, dtype=F32):
    return jax.ShapeDtypeStruct(shape, dtype)


def mask_roots(states, scal, pieces):
    roots, cap, width = states.shape
    step = cap // sum(TWIN)

    def kernel(s_ref, states_ref, own_ref, own_hi, own_lo, other_hi, other_lo, *other_refs):
        row = lax.broadcasted_iota(jnp.int32, (step, width), 0) + pl.program_id(0) * step
        col = lax.broadcasted_iota(jnp.int32, (step, width), 1)
        keep = (row < s_ref[1]) & (col < s_ref[2])
        own = jnp.where(keep, states_ref[s_ref[0]], 0.0)
        own_ref[...] = own
        own_hi[...], own_lo[...] = split(own)
        other = jnp.where(keep, states_ref[1 - s_ref[0]], 0.0)
        other_hi[...], other_lo[...] = split(other)
        first = 0
        for part, ref in zip(TWIN, other_refs):

            @pl.when((pl.program_id(0) >= first) & (pl.program_id(0) < first + part))
            def _():
                ref[...] = other

            first += part

    piece_specs, first = [], 0
    for part in TWIN:
        piece_specs.append(pl.BlockSpec((step, width), lambda s, *_, first=first, part=part: (jnp.clip(s - first, 0, part - 1), 0)))
        first += part
    half = sds((cap, width), BF16)
    own, own_hi, own_lo, other_hi, other_lo, *others = call(
        kernel,
        (sds((cap, width)), half, half, half, half) + tuple(sds((rows, width)) for rows in pieces),
        grid=(sum(TWIN),),
        scalars=1,
        in_specs=[pl.BlockSpec((roots, step, width), lambda s, *_: (0, s, 0))],
        out_specs=(rows_at(step, width),) * 5 + tuple(piece_specs),
        nbytes=4 * states.size * 3,
    )(scal, states)
    return own, (own_hi, own_lo), others, (other_hi, other_lo)


def fetched(kernel, inputs, buffers, outs, results, *, scalars, root=None, passed=(), extra=(), aliases=None, flops=0, mib):
    n_in, n_out = len(inputs), len(outs)
    laid = [k for k, (_, fills) in enumerate(buffers) if len(fills) > 1]
    direct = {k for k, _ in passed}

    def body(s_ref, *refs):
        ins, out_refs, refs = refs[:n_in], refs[n_in : n_in + n_out], refs[n_in + n_out :]
        bufs = dict(zip([k for k in laid if k not in direct], refs))
        rest = refs[len(bufs) :]
        for k, dst in passed:
            bufs[k] = out_refs[dst]

        def lay(k):
            for src, first, rows, to in buffers[k][1]:
                to = pl.multiple_of(to(s_ref), 8) if callable(to) else to
                bufs[k][pl.ds(to, rows), :] = ins[src][pl.ds(first, rows), :]

        def get(k):
            if k not in bufs:
                return ins[buffers[k][1][0][0]][...]
            lay(k)
            return bufs[k][...]

        def put(k, value):
            at = 0
            for dst in results[k][1]:
                rows = outs[dst].shape[-2]
                if root is None:
                    out_refs[dst][...] = value[at : at + rows]
                else:
                    out_refs[dst][0] = value
                at += rows

        def pass_on():
            for k, _ in passed:
                lay(k)

        kernel(get, put, pass_on, s_ref, *rest)

    scratch = [pltpu.VMEM(buffers[k][0], inputs[buffers[k][1][0][0]].dtype) for k in laid if k not in direct]
    used = {fill[0] for _, fills in buffers for fill in fills}
    in_specs = [whole(x.shape) if k in used else pl.BlockSpec(memory_space=pl.ANY) for k, x in enumerate(inputs)]
    if root is None:
        out_specs = tuple(whole(x.shape) for x in outs)
    else:
        out_specs = tuple(pl.BlockSpec((1, *x.shape[1:]), lambda s, s_ref: (root(s_ref), 0, 0)) for x in outs)
    return call(
        body,
        tuple(outs),
        scalars=1,
        in_specs=in_specs,
        out_specs=out_specs,
        scratch=scratch + list(extra),
        flops=flops,
        nbytes=sum(x.size * 4 for x in (*inputs, *outs)),
        aliases=aliases,
        mib=mib,
    )(scalars, *inputs)


class Operands:
    def __init__(self):
        self.inputs = []

    def add(self, array):
        for k, known in enumerate(self.inputs):
            if known is array:
                return k
        self.inputs.append(array)
        return len(self.inputs) - 1

    def stacked(self, *arrays):
        fills, at = [], 0
        for array in arrays:
            fills.append((self.add(array), 0, array.shape[0], at))
            at += array.shape[0]
        return (at, arrays[0].shape[1]), fills

    def placed(self, arrays, unit, first_scalar):
        fills = []
        for array in arrays:
            for sub in range(array.shape[0] // unit):
                at = first_scalar + len(fills)
                fills.append((self.add(array), sub * unit, unit, lambda s_ref, at=at: s_ref[at]))
        return (unit * len(fills), arrays[0].shape[1]), fills


def masked(value, s_ref):
    row = lax.broadcasted_iota(jnp.int32, value.shape, 0)
    col = lax.broadcasted_iota(jnp.int32, value.shape, 1)
    return jnp.where((row < s_ref[1]) & (col < s_ref[2]), value, 0.0)


def hub_out(scal, at_l, pieces, up, own, op_r, next_parts, lo_parts):
    cap, width = up.shape
    n = len(pieces)
    ops = Operands()
    buffers = [
        ops.stacked(op_r),
        ops.stacked(own[0]),
        ops.stacked(own[1]),
        ops.placed(lo_parts, lo_parts[0].shape[0], at_l),
        ops.stacked(up),
        ops.placed(next_parts, next_parts[0].shape[0], at_l),
    ]

    def kernel(get, put, pass_on, s_ref, mid):
        r = split(get(0))
        mid[0], mid[1] = split(dot_nn((get(1), get(2)), r))
        put(0, dot_nn(split(get(3).T), (mid[0], mid[1])))
        mid[2], mid[3] = split(dot_nt(split(get(4)), r))
        put(1, dot_nn(split(get(5)), (mid[2], mid[3])))

    got = fetched(
        kernel,
        ops.inputs,
        buffers,
        [sds((rows, width)) for rows in pieces] * 2,
        [((cap, width), list(range(n))), ((cap, width), list(range(n, 2 * n)))],
        scalars=scal,
        extra=[pltpu.VMEM((4, cap, width), BF16)],
        flops=24 * cap * cap * width,
        mib=30,
    )
    return got[n:], got[:n]


def joined(scal, parts, at=None, unit=None):
    ops = Operands()
    buffers = [ops.stacked(*parts) if at is None else ops.placed(parts, unit, at)]
    return fetched(
        lambda get, put, pass_on, s_ref: pass_on(),
        ops.inputs,
        buffers,
        [sds(buffers[0][0])],
        [],
        scalars=scal,
        passed=[(0, 0)],
        mib=8,
    )[0]


def right_product(scal, piece, op_r):
    ops = Operands()
    buffers = [ops.stacked(op_r), ops.stacked(piece)]

    def kernel(get, put, pass_on, s_ref):
        put(0, dot_nn(split(get(1)), split(get(0))))

    return fetched(
        kernel,
        ops.inputs,
        buffers,
        [sds(piece.shape)],
        [(piece.shape, [0])],
        scalars=scal,
        flops=6 * piece.size * piece.shape[1],
        mib=16,
    )[0]


def own_hop(scal, at_l, hop_in, op_r, lo_parts, own_sum):
    cap, width = own_sum.shape
    ops = Operands()
    buffers = [
        ops.stacked(op_r),
        ops.stacked(*hop_in),
        ops.placed(lo_parts, lo_parts[0].shape[0], at_l),
        ops.stacked(own_sum),
    ]

    def kernel(get, put, pass_on, s_ref, mid):
        mid[0], mid[1] = split(dot_nt(split(get(1)), split(get(0))))
        put(0, get(3) + dot_nn(split(get(2)), (mid[0], mid[1])))

    return fetched(
        kernel,
        ops.inputs,
        buffers,
        [sds((cap, width))],
        [((cap, width), [0])],
        scalars=scal,
        extra=[pltpu.VMEM((2, cap, width), BF16)],
        flops=12 * cap * cap * width,
        mib=26,
    )[0]


def own_back(scal, at_l, shape, back_mid, next_parts, own_sum):
    _, cap, width = shape
    ops = Operands()
    buffers = [
        ops.stacked(*back_mid),
        ops.placed(next_parts, next_parts[0].shape[0], at_l),
        ops.stacked(own_sum),
    ]

    def kernel(get, put, pass_on, s_ref):
        put(0, masked(dot_nn(split(get(1).T), split(get(0))) + get(2), s_ref))

    return fetched(
        kernel,
        ops.inputs,
        buffers,
        [sds(shape)],
        [((cap, width), [0])],
        scalars=scal,
        root=lambda s_ref: s_ref[0],
        flops=6 * cap * cap * width,
        mib=24,
    )[0]


def left_local(scal, at_l, le_parts, own, other):
    cap, width = own[0].shape
    ops = Operands()
    buffers = [ops.placed(le_parts, le_parts[0].shape[0], at_l)] + [ops.stacked(x) for x in (*own, *other)]

    def kernel(get, put, pass_on, s_ref):
        a = split(get(0))
        put(0, dot_nn(a, (get(1), get(2))))
        put(1, dot_nn(a, (get(3), get(4))))

    return fetched(
        kernel,
        ops.inputs,
        buffers,
        [sds((cap, width))] * 2,
        [((cap, width), [k]) for k in range(2)],
        scalars=scal,
        flops=12 * cap * cap * width,
        mib=24,
    )


def right_local(scal, at_r, halves, unit, own, other, sums):
    cap, width = own[0].shape
    ops = Operands()
    buffers = [ops.placed(halves, unit, at_r)] + [ops.stacked(x) for x in (*own, *other, *sums)]

    def kernel(get, put, pass_on, s_ref):
        r = split(get(0))
        value = dot_nt((get(1), get(2)), r)
        put(0, get(5) + value)
        value = dot_nt((get(3), get(4)), r)
        put(1, get(6) + value)

    return fetched(
        kernel,
        ops.inputs,
        buffers,
        [sds((cap, width))] * 2,
        [((cap, width), [k]) for k in range(2)],
        scalars=scal,
        flops=12 * cap * width * width,
        mib=26,
    )


def combine(mine, hop, hop_far, back_far):
    def kernel(s_ref, a, b, c, out):
        out[...] = jnp.where(s_ref[0] == 0, a[...], b[...]) + c[...]

    return call(
        kernel,
        sds(hop.shape),
        scalars=1,
        in_specs=[whole(hop.shape)] * 3,
        out_specs=whole(hop.shape),
        nbytes=16 * hop.size,
    )(mine[None], hop, hop_far, back_far)


def finish(partial, scal, other_sum, returned):
    ops = Operands()
    buffers = [ops.stacked(other_sum), ops.stacked(*returned)]
    place = ops.add(partial)

    def kernel(get, put, pass_on, s_ref):
        total = get(0)
        put(0, masked(total + get(1), s_ref))

    return fetched(
        kernel,
        ops.inputs,
        buffers,
        [sds(partial.shape)],
        [(other_sum.shape, [0])],
        scalars=scal,
        root=lambda s_ref: 1 - s_ref[0],
        aliases={1 + place: 0},
        mib=12,
    )[0]


def on_device(n_l, n_r, states, left_env, right_env, left_op, right_op, sizes_left, sizes_right):
    cap = states.shape[1]
    i, j = lax.axis_index("lsec"), lax.axis_index("rsec")
    mine = (i % 2).astype(jnp.int32)
    sizes = (sizes_left[0], sizes_right[0])

    def move(value, to):
        pairs = []
        for a in range(n_l):
            for b in range(n_r):
                goal = to(a, b)
                if goal is not None and 0 <= goal[0] < n_l and 0 <= goal[1] < n_r:
                    pairs.append((a * n_r + b, goal[0] * n_r + goal[1]))
        return lax.ppermute(value, AXES, pairs)

    def swap(value):
        return move(value, lambda a, b: (a ^ 1, b))

    def spread_left(shard):
        held = {0: shard}
        bit = n_r // 2
        while bit:
            for m in list(held):
                held[m ^ bit] = move(held[m], lambda a, b: (a, b ^ bit))
            bit //= 2
        return held

    def spread_right(shard):
        return [shard] + [move(shard, lambda a, b: ((a + 2 * k) % n_l, b)) for k in range(1, n_l // 2)]

    lo, le = left_op[0], left_env[0]
    ro, re = right_op[0], right_env[0]
    rows_l, rows_r = lo.shape[0], ro.shape[0]

    def right_rows(base):
        return [((base - 2 * k) % n_l) * rows_r for k in range(n_l // 2)]

    next_lo = move(lo, lambda a, b: (a - 1, b))
    all_lo, all_le, all_n = spread_left(lo), spread_left(le), spread_left(next_lo)
    keys = list(all_lo)
    all_lo, all_le, all_n = ([held[m] for m in keys] for held in (all_lo, all_le, all_n))
    left_rows = [(j ^ m) * rows_l for m in keys]
    own_rows, twin_rows = right_rows(i), right_rows(i ^ 1)
    paired = [row for pair in zip(own_rows, twin_rows) for row in pair]
    scal = jnp.stack([mine, *sizes, *left_rows, *own_rows, *twin_rows, *paired]).astype(jnp.int32)
    at_l, at_r, at_e = 3, 3 + n_r, 3 + n_r + n_l

    twin_pieces = [cap * part // sum(TWIN) for part in TWIN]
    own, own_split, other, other_split = mask_roots(states, scal, twin_pieces)
    twin = [swap(piece) for piece in other]
    half_r = joined(scal, spread_right(ro))
    all_e = spread_right(joined(scal, [re, swap(re)]))
    up = move(own, lambda a, b: (a, b - 1))
    op_r = joined(scal, [half_r, swap(half_r)], at_r, rows_r)
    twin_hop = [move(v, lambda a, b: (a if a % 2 else a + 2, b - 1)) for v in twin]
    twin_mid = [right_product(scal, v, op_r) for v in twin]
    twin_mid = [move(v, lambda a, b: (a - 2 if a % 2 else a, b + 1)) for v in twin_mid]

    pieces = [cap * part // sum(RETURNS) for part in RETURNS]
    hops, backs = hub_out(scal, at_l, pieces, up, own_split, op_r, all_n, all_lo)
    returned = []
    for hop, back in zip(hops, backs):
        hop_far = move(hop, lambda a, b: (a + 2, b) if a % 2 else None)
        back_far = move(back, lambda a, b: (a if a % 2 else a - 2, b + 1))
        returned.append(swap(combine(mine, hop, hop_far, back_far)))

    sums = left_local(scal, at_l, all_le, own_split, other_split)
    own_sum, other_sum = right_local(scal, at_e, all_e, rows_r, own_split, other_split, sums)
    own_sum = own_hop(scal, at_l, twin_hop, op_r, all_lo, own_sum)
    partial = own_back(scal, at_l, states.shape, twin_mid, all_n, own_sum)
    return finish(partial, scal, other_sum, returned)


def solution(mesh):
    in_specs = (
        P(None, "lsec", "rsec"),
        P("lsec", "rsec", None),
        P("rsec", "lsec", None),
        P("lsec", "rsec", None),
        P("rsec", "lsec", None),
        P("lsec"),
        P("rsec"),
    )
    n_l, n_r = mesh.shape["lsec"], mesh.shape["rsec"]

    def body(*args):
        return on_device(n_l, n_r, *args)

    return jax.shard_map(
        body, mesh=mesh, in_specs=in_specs, out_specs=P(None, "lsec", "rsec"), check_vma=False
    )
```

```python
import jax
import jax.numpy as jnp
from jax import lax
from jax.experimental import pallas as pl
from jax.experimental.pallas import tpu as pltpu
from jax.sharding import PartitionSpec as P

AXES = ("lsec", "rsec")
RETURNS = (2, 2, 1)
TWIN = (2, 3)
F32, BF16 = jnp.float32, jnp.bfloat16
MIB = 1024 * 1024


def split(x):
    hi = x.astype(BF16)
    return hi, (x - hi.astype(F32)).astype(BF16)


def dot_nn(a, b):
    left = jnp.concatenate([a[0], a[0], a[1]], axis=1)
    right = jnp.concatenate([b[0], b[1], b[0]], axis=0)
    return lax.dot_general(left, right, (((1,), (0,)), ((), ())), preferred_element_type=F32)


def dot_nt(a, b):
    left = jnp.concatenate([a[0], a[0], a[1]], axis=1)
    right = jnp.concatenate([b[0], b[1], b[0]], axis=1)
    return lax.dot_general(left, right, (((1,), (1,)), ((), ())), preferred_element_type=F32)


def call(kernel, out_shape, *, grid=(1,), scalars=0, in_specs, out_specs, scratch=(), flops=0, nbytes=0, aliases=None, mib=12):
    return pl.pallas_call(
        kernel,
        out_shape=out_shape,
        grid_spec=pltpu.PrefetchScalarGridSpec(
            num_scalar_prefetch=scalars, grid=grid, in_specs=in_specs, out_specs=out_specs, scratch_shapes=scratch
        ),
        compiler_params=pltpu.CompilerParams(vmem_limit_bytes=mib * MIB),
        cost_estimate=pl.CostEstimate(flops=flops, bytes_accessed=nbytes, transcendentals=0),
        input_output_aliases=aliases or {},
    )


def whole(shape):
    return pl.BlockSpec(shape, lambda *_: (0,) * len(shape))


def rows_at(chunk, width):
    return pl.BlockSpec((chunk, width), lambda s, *_: (s, 0))


def sds(shape, dtype=F32):
    return jax.ShapeDtypeStruct(shape, dtype)


def mask_roots(states, scal, pieces):
    roots, cap, width = states.shape
    step = cap // sum(TWIN)

    def kernel(s_ref, states_ref, own_ref, own_hi, own_lo, other_hi, other_lo, *other_refs):
        row = lax.broadcasted_iota(jnp.int32, (step, width), 0) + pl.program_id(0) * step
        col = lax.broadcasted_iota(jnp.int32, (step, width), 1)
        keep = (row < s_ref[1]) & (col < s_ref[2])
        own = jnp.where(keep, states_ref[s_ref[0]], 0.0)
        own_ref[...] = own
        own_hi[...], own_lo[...] = split(own)
        other = jnp.where(keep, states_ref[1 - s_ref[0]], 0.0)
        other_hi[...], other_lo[...] = split(other)
        first = 0
        for part, ref in zip(TWIN, other_refs):

            @pl.when((pl.program_id(0) >= first) & (pl.program_id(0) < first + part))
            def _():
                ref[...] = other

            first += part

    piece_specs, first = [], 0
    for part in TWIN:
        piece_specs.append(pl.BlockSpec((step, width), lambda s, *_, first=first, part=part: (jnp.clip(s - first, 0, part - 1), 0)))
        first += part
    half = sds((cap, width), BF16)
    own, own_hi, own_lo, other_hi, other_lo, *others = call(
        kernel,
        (sds((cap, width)), half, half, half, half) + tuple(sds((rows, width)) for rows in pieces),
        grid=(sum(TWIN),),
        scalars=1,
        in_specs=[pl.BlockSpec((roots, step, width), lambda s, *_: (0, s, 0))],
        out_specs=(rows_at(step, width),) * 5 + tuple(piece_specs),
        nbytes=4 * states.size * 3,
    )(scal, states)
    return own, (own_hi, own_lo), others, (other_hi, other_lo)


def fetched(kernel, inputs, buffers, outs, results, *, scalars, root=None, passed=(), extra=(), aliases=None, flops=0, mib):
    n_in, n_out = len(inputs), len(outs)
    laid = [k for k, (_, fills) in enumerate(buffers) if len(fills) > 1]
    direct = {k for k, _ in passed}

    def body(s_ref, *refs):
        ins, out_refs, refs = refs[:n_in], refs[n_in : n_in + n_out], refs[n_in + n_out :]
        bufs = dict(zip([k for k in laid if k not in direct], refs))
        rest = refs[len(bufs) :]
        for k, dst in passed:
            bufs[k] = out_refs[dst]

        def lay(k):
            for src, first, rows, to in buffers[k][1]:
                to = pl.multiple_of(to(s_ref), 8) if callable(to) else to
                bufs[k][pl.ds(to, rows), :] = ins[src][pl.ds(first, rows), :]

        def get(k):
            if k not in bufs:
                return ins[buffers[k][1][0][0]][...]
            lay(k)
            return bufs[k][...]

        def put(k, value):
            at = 0
            for dst in results[k][1]:
                rows = outs[dst].shape[-2]
                if root is None:
                    out_refs[dst][...] = value[at : at + rows]
                else:
                    out_refs[dst][0] = value
                at += rows

        def pass_on():
            for k, _ in passed:
                lay(k)

        kernel(get, put, pass_on, s_ref, *rest)

    scratch = [pltpu.VMEM(buffers[k][0], inputs[buffers[k][1][0][0]].dtype) for k in laid if k not in direct]
    used = {fill[0] for _, fills in buffers for fill in fills}
    in_specs = [whole(x.shape) if k in used else pl.BlockSpec(memory_space=pl.ANY) for k, x in enumerate(inputs)]
    if root is None:
        out_specs = tuple(whole(x.shape) for x in outs)
    else:
        out_specs = tuple(pl.BlockSpec((1, *x.shape[1:]), lambda s, s_ref: (root(s_ref), 0, 0)) for x in outs)
    return call(
        body,
        tuple(outs),
        scalars=1,
        in_specs=in_specs,
        out_specs=out_specs,
        scratch=scratch + list(extra),
        flops=flops,
        nbytes=sum(x.size * 4 for x in (*inputs, *outs)),
        aliases=aliases,
        mib=mib,
    )(scalars, *inputs)


class Operands:
    def __init__(self):
        self.inputs = []

    def add(self, array):
        for k, known in enumerate(self.inputs):
            if known is array:
                return k
        self.inputs.append(array)
        return len(self.inputs) - 1

    def stacked(self, *arrays):
        fills, at = [], 0
        for array in arrays:
            fills.append((self.add(array), 0, array.shape[0], at))
            at += array.shape[0]
        return (at, arrays[0].shape[1]), fills

    def placed(self, arrays, unit, first_scalar):
        fills = []
        for array in arrays:
            for sub in range(array.shape[0] // unit):
                at = first_scalar + len(fills)
                fills.append((self.add(array), sub * unit, unit, lambda s_ref, at=at: s_ref[at]))
        return (unit * len(fills), arrays[0].shape[1]), fills


def masked(value, s_ref):
    row = lax.broadcasted_iota(jnp.int32, value.shape, 0)
    col = lax.broadcasted_iota(jnp.int32, value.shape, 1)
    return jnp.where((row < s_ref[1]) & (col < s_ref[2]), value, 0.0)


def hub_out(scal, at_l, pieces, up, own, op_r, next_parts, lo_parts):
    cap, width = up.shape
    n = len(pieces)
    ops = Operands()
    buffers = [
        ops.stacked(op_r),
        ops.stacked(own[0]),
        ops.stacked(own[1]),
        ops.placed(lo_parts, lo_parts[0].shape[0], at_l),
        ops.stacked(up),
        ops.placed(next_parts, next_parts[0].shape[0], at_l),
    ]

    def kernel(get, put, pass_on, s_ref, mid):
        r = split(get(0))
        mid[0], mid[1] = split(dot_nn((get(1), get(2)), r))
        put(0, dot_nn(split(get(3).T), (mid[0], mid[1])))
        mid[2], mid[3] = split(dot_nt(split(get(4)), r))
        put(1, dot_nn(split(get(5)), (mid[2], mid[3])))

    got = fetched(
        kernel,
        ops.inputs,
        buffers,
        [sds((rows, width)) for rows in pieces] * 2,
        [((cap, width), list(range(n))), ((cap, width), list(range(n, 2 * n)))],
        scalars=scal,
        extra=[pltpu.VMEM((4, cap, width), BF16)],
        flops=24 * cap * cap * width,
        mib=30,
    )
    return got[n:], got[:n]


def joined(scal, parts, at=None, unit=None):
    ops = Operands()
    buffers = [ops.stacked(*parts) if at is None else ops.placed(parts, unit, at)]
    return fetched(
        lambda get, put, pass_on, s_ref: pass_on(),
        ops.inputs,
        buffers,
        [sds(buffers[0][0])],
        [],
        scalars=scal,
        passed=[(0, 0)],
        mib=8,
    )[0]


def right_product(scal, piece, op_r):
    ops = Operands()
    buffers = [ops.stacked(op_r), ops.stacked(piece)]

    def kernel(get, put, pass_on, s_ref):
        put(0, dot_nn(split(get(1)), split(get(0))))

    return fetched(
        kernel,
        ops.inputs,
        buffers,
        [sds(piece.shape)],
        [(piece.shape, [0])],
        scalars=scal,
        flops=6 * piece.size * piece.shape[1],
        mib=16,
    )[0]


def own_hop(scal, at_l, hop_in, op_r, lo_parts, own_sum):
    cap, width = own_sum.shape
    ops = Operands()
    buffers = [
        ops.stacked(op_r),
        ops.stacked(*hop_in),
        ops.placed(lo_parts, lo_parts[0].shape[0], at_l),
        ops.stacked(own_sum),
    ]

    def kernel(get, put, pass_on, s_ref, mid):
        mid[0], mid[1] = split(dot_nt(split(get(1)), split(get(0))))
        put(0, get(3) + dot_nn(split(get(2)), (mid[0], mid[1])))

    return fetched(
        kernel,
        ops.inputs,
        buffers,
        [sds((cap, width))],
        [((cap, width), [0])],
        scalars=scal,
        extra=[pltpu.VMEM((2, cap, width), BF16)],
        flops=12 * cap * cap * width,
        mib=26,
    )[0]


def own_back(scal, at_l, shape, back_mid, next_parts, own_sum):
    _, cap, width = shape
    ops = Operands()
    buffers = [
        ops.stacked(*back_mid),
        ops.placed(next_parts, next_parts[0].shape[0], at_l),
        ops.stacked(own_sum),
    ]

    def kernel(get, put, pass_on, s_ref):
        put(0, masked(dot_nn(split(get(1).T), split(get(0))) + get(2), s_ref))

    return fetched(
        kernel,
        ops.inputs,
        buffers,
        [sds(shape)],
        [((cap, width), [0])],
        scalars=scal,
        root=lambda s_ref: s_ref[0],
        flops=6 * cap * cap * width,
        mib=24,
    )[0]


def left_local(scal, at_l, le_parts, own, other):
    cap, width = own[0].shape
    ops = Operands()
    buffers = [ops.placed(le_parts, le_parts[0].shape[0], at_l)] + [ops.stacked(x) for x in (*own, *other)]

    def kernel(get, put, pass_on, s_ref):
        a = split(get(0))
        put(0, dot_nn(a, (get(1), get(2))))
        put(1, dot_nn(a, (get(3), get(4))))

    return fetched(
        kernel,
        ops.inputs,
        buffers,
        [sds((cap, width))] * 2,
        [((cap, width), [k]) for k in range(2)],
        scalars=scal,
        flops=12 * cap * cap * width,
        mib=24,
    )


def right_local(scal, at_r, halves, unit, own, other, sums):
    cap, width = own[0].shape
    ops = Operands()
    buffers = [ops.placed(halves, unit, at_r)] + [ops.stacked(x) for x in (*own, *other, *sums)]

    def kernel(get, put, pass_on, s_ref):
        r = split(get(0))
        value = dot_nt((get(1), get(2)), r)
        put(0, get(5) + value)
        value = dot_nt((get(3), get(4)), r)
        put(1, get(6) + value)

    return fetched(
        kernel,
        ops.inputs,
        buffers,
        [sds((cap, width))] * 2,
        [((cap, width), [k]) for k in range(2)],
        scalars=scal,
        flops=12 * cap * width * width,
        mib=26,
    )


def combine(mine, hop, hop_far, back_far):
    def kernel(s_ref, a, b, c, out):
        out[...] = jnp.where(s_ref[0] == 0, a[...], b[...]) + c[...]

    return call(
        kernel,
        sds(hop.shape),
        scalars=1,
        in_specs=[whole(hop.shape)] * 3,
        out_specs=whole(hop.shape),
        nbytes=16 * hop.size,
    )(mine[None], hop, hop_far, back_far)


def finish(partial, scal, other_sum, returned, first):
    _, _, width = partial.shape
    rows = sum(x.shape[0] for x in returned)
    n = len(returned)

    def kernel(s_ref, _, other_ref, *refs):
        at = 0
        for piece in refs[:n]:
            span = pl.ds(at, piece.shape[0])
            row = lax.broadcasted_iota(jnp.int32, piece.shape, 0) + first + at
            col = lax.broadcasted_iota(jnp.int32, piece.shape, 1)
            total = other_ref[span, :] + piece[...]
            refs[n][0, span, :] = jnp.where((row < s_ref[1]) & (col < s_ref[2]), total, 0.0)
            at += piece.shape[0]

    return call(
        kernel,
        sds(partial.shape),
        scalars=1,
        in_specs=[pl.BlockSpec(memory_space=pl.ANY), pl.BlockSpec((rows, width), lambda *_: (first // rows, 0))]
        + [whole(x.shape) for x in returned],
        out_specs=pl.BlockSpec((1, rows, width), lambda s, s_ref: (1 - s_ref[0], first // rows, 0)),
        nbytes=12 * rows * width,
        aliases={1: 0},
    )(scal, partial, other_sum, *returned)


def on_device(n_l, n_r, states, left_env, right_env, left_op, right_op, sizes_left, sizes_right):
    cap = states.shape[1]
    i, j = lax.axis_index("lsec"), lax.axis_index("rsec")
    mine = (i % 2).astype(jnp.int32)
    sizes = (sizes_left[0], sizes_right[0])

    def move(value, to):
        pairs = []
        for a in range(n_l):
            for b in range(n_r):
                goal = to(a, b)
                if goal is not None and 0 <= goal[0] < n_l and 0 <= goal[1] < n_r:
                    pairs.append((a * n_r + b, goal[0] * n_r + goal[1]))
        return lax.ppermute(value, AXES, pairs)

    def swap(value):
        return move(value, lambda a, b: (a ^ 1, b))

    def spread_left(shard):
        held = {0: shard}
        bit = n_r // 2
        while bit:
            for m in list(held):
                held[m ^ bit] = move(held[m], lambda a, b: (a, b ^ bit))
            bit //= 2
        return held

    def spread_right(shard):
        return [shard] + [move(shard, lambda a, b: ((a + 2 * k) % n_l, b)) for k in range(1, n_l // 2)]

    lo, le = left_op[0], left_env[0]
    ro, re = right_op[0], right_env[0]
    rows_l, rows_r = lo.shape[0], ro.shape[0]

    def right_rows(base):
        return [((base - 2 * k) % n_l) * rows_r for k in range(n_l // 2)]

    next_lo = move(lo, lambda a, b: (a - 1, b))
    all_lo, all_le, all_n = spread_left(lo), spread_left(le), spread_left(next_lo)
    keys = list(all_lo)
    all_lo, all_le, all_n = ([held[m] for m in keys] for held in (all_lo, all_le, all_n))
    left_rows = [(j ^ m) * rows_l for m in keys]
    own_rows, twin_rows = right_rows(i), right_rows(i ^ 1)
    paired = [row for pair in zip(own_rows, twin_rows) for row in pair]
    scal = jnp.stack([mine, *sizes, *left_rows, *own_rows, *twin_rows, *paired]).astype(jnp.int32)
    at_l, at_r, at_e = 3, 3 + n_r, 3 + n_r + n_l

    twin_pieces = [cap * part // sum(TWIN) for part in TWIN]
    own, own_split, other, other_split = mask_roots(states, scal, twin_pieces)
    twin = [swap(piece) for piece in other]
    half_r = joined(scal, spread_right(ro))
    all_e = spread_right(joined(scal, [re, swap(re)]))
    up = move(own, lambda a, b: (a, b - 1))
    op_r = joined(scal, [half_r, swap(half_r)], at_r, rows_r)
    twin_hop = [move(v, lambda a, b: (a if a % 2 else a + 2, b - 1)) for v in twin]
    twin_mid = [right_product(scal, v, op_r) for v in twin]
    twin_mid = [move(v, lambda a, b: (a - 2 if a % 2 else a, b + 1)) for v in twin_mid]

    pieces = [cap * part // sum(RETURNS) for part in RETURNS]
    hops, backs = hub_out(scal, at_l, pieces, up, own_split, op_r, all_n, all_lo)
    returned = []
    for hop, back in zip(hops, backs):
        hop_far = move(hop, lambda a, b: (a + 2, b) if a % 2 else None)
        back_far = move(back, lambda a, b: (a if a % 2 else a - 2, b + 1))
        returned.append(swap(combine(mine, hop, hop_far, back_far)))

    sums = left_local(scal, at_l, all_le, own_split, other_split)
    own_sum, other_sum = right_local(scal, at_e, all_e, rows_r, own_split, other_split, sums)
    own_sum = own_hop(scal, at_l, twin_hop, op_r, all_lo, own_sum)
    partial = own_back(scal, at_l, states.shape, twin_mid, all_n, own_sum)
    partial = finish(partial, scal, other_sum, returned[:-1], 0)
    return finish(partial, scal, other_sum, returned[-1:], cap - pieces[-1])


def solution(mesh):
    in_specs = (
        P(None, "lsec", "rsec"),
        P("lsec", "rsec", None),
        P("rsec", "lsec", None),
        P("lsec", "rsec", None),
        P("rsec", "lsec", None),
        P("lsec"),
        P("rsec"),
    )
    n_l, n_r = mesh.shape["lsec"], mesh.shape["rsec"]

    def body(*args):
        return on_device(n_l, n_r, *args)

    return jax.shard_map(
        body, mesh=mesh, in_specs=in_specs, out_specs=P(None, "lsec", "rsec"), check_vma=False
    )
```
